32 devices in a mesh: lat: 4 (over x, core), src: 8 (over z, y).
Axes of the slice: x: 2, y: 2, z: 4, core: 2. Of those that a mesh axis runs over, the one named last changes fastest.
Arguments:
- fine_residual: bfloat16 [8, 16, 256, 2048], P('lat', 'src'), may hold values from -6 to 6
- basis: bfloat16 [8, 16, 2048, 128], P('lat', 'src'), may hold values from -0.25 to 0.25
- diag_inverse: bfloat16 [8, 16, 128, 128], P('lat', 'src'), may hold values from -0.32 to 1.7, as said below
- hoppings: bfloat16 [8, 16, 8, 128, 128], P('lat', 'src'), may hold values from -0.125 to 0.125
- neighbours: int32 [16, 6], replicated, may hold values from 0 to 15, as said below
- aggregation: int32 [8, 16], P('lat', 'src'), may hold values from 0 to 15, as said below
Outputs:
- correction: bfloat16 [8, 16, 256, 2048], P('lat', 'src')
The draws below stay inside these ranges and needn't reach their ends.
Inputs may be any that keep to these rules, and one draw needn't show every extreme that they name: `diag_inverse`: a site's diagonal inverse is one on the diagonal within a fifth (two fifths in some draws) plus independent off-diagonal entries. The spatial sites form a periodic grid of 8 by 1 by 2 sites, site (x, y, z) having index (x * 1 + y) * 2 + z; columns 2k and 2k+1 hold the two periodic neighbours along grid direction k, one step up and one step down, in an order drawn for each k. `aggregation`: in each row, every aligned block of 2 entries is a permutation of that block's own column indices.
All inputs are finite; a program needn't handle non-finite values.
Results may differ from the reference program's by a relative error of at most 0.0075.
Values may be sent and summed in bfloat16 or wider, within the bound.
A program may use at most 128 MiB of HBM per device.

```python
import math
import jax
import jax.numpy as jnp
from jax import lax

FINE = 2048
CDOF = 128
NSRC = 256
SWEEPS = 3
SP_DEV = 2
NT = 8
SPACE = 16


def draw_diag_inverse(key, part):
    first_key, second_key = jax.random.split(key)
    identity = jnp.eye(CDOF, dtype=jnp.float32)
    off_diag = jnp.clip(jax.random.normal(first_key, (NT, SPACE, CDOF, CDOF), jnp.float32) * (0.5 / math.sqrt(CDOF)), -0.3, 0.3)
    diag_part = jax.random.uniform(second_key, (NT, SPACE, 1, 1), jnp.float32, 0.8, 1.2)
    return (off_diag * (1.0 - identity) + diag_part * identity).astype(jnp.bfloat16)


def grid_index(x_pos, y_pos, z_pos, y_len):
    return ((x_pos * y_len + y_pos) * 2 + z_pos).astype(jnp.int32)


def draw_neighbours(key, part):
    flips = jax.random.randint(jax.random.fold_in(key, 17), (3,), 0, 2).astype(jnp.int32)
    x_len = SPACE // SP_DEV
    y_len = SP_DEV // 2
    sites = jnp.arange(SPACE, dtype=jnp.int32)
    z_pos = sites % 2
    y_pos = sites // 2 % y_len
    x_pos = sites // SP_DEV
    pairs = [(grid_index((x_pos + 1) % x_len, y_pos, z_pos, y_len), grid_index((x_pos + x_len - 1) % x_len, y_pos, z_pos, y_len)), (grid_index(x_pos, (y_pos + 1) % y_len, z_pos, y_len), grid_index(x_pos, (y_pos + y_len - 1) % y_len, z_pos, y_len)), (grid_index(x_pos, y_pos, (z_pos + 1) % 2, y_len), grid_index(x_pos, y_pos, (z_pos + 1) % 2, y_len))]
    columns = []
    for direction in range(3):
        upward, downward = pairs[direction]
        flipped = flips[direction] == 1
        columns.append(jnp.where(flipped, downward, upward))
        columns.append(jnp.where(flipped, upward, downward))
    return jnp.stack(columns, axis=1).astype(jnp.int32)


def draw_aggregation(key, part):
    blocks = SPACE // SP_DEV
    subkeys = jax.random.split(key, NT * blocks)
    within = jax.vmap(lambda single: jax.random.permutation(single, SP_DEV))(subkeys).astype(jnp.int32)
    offsets = jnp.arange(NT * blocks, dtype=jnp.int32) % blocks * SP_DEV
    return (within + offsets[:, None]).reshape(NT, SPACE)


def block_scale(key, dims, shards, least, largest):
    gain = 1.0
    for axis_at, shards_of in shards:
        draws = jax.random.uniform(jax.random.fold_in(jax.random.fold_in(key, 6), axis_at), (shards_of,), jnp.float32, least / len(shards), largest / len(shards))
        gain = gain * jnp.repeat(jnp.exp(draws), dims[axis_at] // shards_of).reshape((-1,) + (1,) * (len(dims) - 1 - axis_at))
    return gain


def noise(key, dims, deviation, bound, cuts=(), held_as=jnp.bfloat16):
    entries = jax.random.normal(key, dims, jnp.float32) * deviation
    if len(cuts) > 0:
        entries = block_scale(key, dims, cuts, -0.22, 0.18) * entries
    return jnp.clip(entries, min=-bound, max=bound).astype(held_as)


def setup_inputs(seed: int = 0) -> dict:
    streams_of = jax.random.split(jax.random.key(seed), 7)
    return {
        "fine_residual": noise(streams_of[0], (NT, SPACE, NSRC, FINE), 1.0, 6.0, ((0, 4), (1, 8))),
        "basis": noise(streams_of[1], (NT, SPACE, FINE, CDOF), (FINE // 4) ** -0.5, 0.25, ((0, 4), (1, 8))),
        "diag_inverse": draw_diag_inverse(jax.random.fold_in(streams_of[6], 71), 0),
        "hoppings": noise(streams_of[3], (NT, SPACE, 8, CDOF, CDOF), (16 * CDOF) ** -0.5, 0.125, ((0, 4), (1, 8))),
        "neighbours": draw_neighbours(jax.random.fold_in(streams_of[6], 71), 0),
        "aggregation": draw_aggregation(jax.random.fold_in(streams_of[6], 71), 0),
    }


damping = 0.8


def hop_sum(iterate, hoppings, neighbours, slices):
    def per_slice(slice_index):
        current = iterate[slice_index]
        spatial = jnp.take(current, neighbours, axis=0)
        upper_time = iterate[(slice_index + 1) % NT]
        lower_time = iterate[(slice_index + NT - 1) % NT]
        stacked = jnp.concatenate([spatial, upper_time[:, None], lower_time[:, None]], axis=1).astype(jnp.float32)
        return jnp.einsum('sknc,skcd->snd', stacked, hoppings[slice_index].astype(jnp.float32))
    return lax.map(per_slice, slices)


def reference(fine_residual, basis, diag_inverse, hoppings, neighbours, aggregation):
    slices = jnp.arange(NT, dtype=jnp.int32)

    def restrict_slice(slice_index):
        return jnp.einsum('snr,src->snc', fine_residual[slice_index].astype(jnp.float32), basis[slice_index].astype(jnp.float32)).astype(jnp.bfloat16)

    restricted = lax.map(restrict_slice, slices)
    inverse = jnp.argsort(aggregation, axis=1).astype(jnp.int32)
    coarse_rhs = jnp.take_along_axis(restricted, inverse[:, :, None, None], axis=1)
    inverse_blocks = diag_inverse.astype(jnp.float32)
    applied = jnp.einsum('tsnc,tscd->tsnd', coarse_rhs.astype(jnp.float32), inverse_blocks)
    iterate = (damping * applied).astype(jnp.bfloat16)
    for sweep_index in range(SWEEPS - 1):
        hop_terms = hop_sum(iterate, hoppings, neighbours, slices)
        difference = (coarse_rhs.astype(jnp.float32) - hop_terms).astype(jnp.bfloat16)
        applied = jnp.einsum('tsnc,tscd->tsnd', difference.astype(jnp.float32), inverse_blocks)
        iterate = ((1.0 - damping) * iterate.astype(jnp.float32) + damping * applied).astype(jnp.bfloat16)
    gathered = jnp.take_along_axis(iterate, aggregation[:, :, None, None], axis=1)

    def prolong_slice(slice_index):
        return jnp.einsum('snc,src->snr', gathered[slice_index].astype(jnp.float32), basis[slice_index].astype(jnp.float32)).astype(jnp.bfloat16)

    return lax.map(prolong_slice, slices)
```

```python
import functools

import jax
import jax.numpy as jnp
from jax import lax
from jax.experimental import pallas as pl
from jax.experimental.pallas import tpu as pltpu
from jax.sharding import PartitionSpec as P

SWEEPS = 3
DAMPING = 0.8
CHUNKS = 4
LAG = 4
F32 = jnp.float32
BF16 = jnp.bfloat16


def dot(a, b):
    return jnp.dot(a, b, preferred_element_type=F32)


def sweep_kernel(
    chunks, lats, srcs, fine, basis, diag, hops, table, agg, out,
    fine_v, basis_v, diag_v, hops_v, rhs, acc, cells, from_partner, from_far, above, below, last,
    fine_sem, basis_sem, diag_sem, hops_sem, out_sem,
    partner_send, partner_recv, far_send, far_recv, above_send, above_recv, below_send, below_recv,
):
    times, sites, sources, _ = fine.shape
    rows = sources // chunks
    lat, src = lax.axis_index("lat"), lax.axis_index("src")
    later, earlier = lax.rem(lat + 1, lats), lax.rem(lat + lats - 1, lats)
    odd = lax.rem(src, 2)
    partner = src + 1 - 2 * odd
    far_target = lax.rem(src + 2 - 4 * odd + srcs, srcs)
    far_source = lax.rem(src - 2 + 4 * odd + srcs, srcs)

    barrier = pltpu.get_barrier_semaphore()
    for device in ((later, src), (earlier, src), (lat, partner), (lat, far_source)):
        pl.semaphore_signal(barrier, inc=1, device_id=device, device_id_type=pl.DeviceIdType.MESH)

    def span(c):
        return pl.ds(c * rows, rows)

    def load_fine(c, t, s):
        return pltpu.make_async_copy(
            fine.at[t, s, span(c)], fine_v.at[t, s, span(c)], fine_sem.at[c, t, s])

    def load_basis(t, s):
        return pltpu.make_async_copy(basis.at[t, s], basis_v.at[t, s], basis_sem.at[t, s])

    load_diag = pltpu.make_async_copy(diag, diag_v, diag_sem)
    load_hops = pltpu.make_async_copy(hops, hops_v, hops_sem)

    pieces = [(c, t) for c in range(chunks) for t in range(times)]
    for c, t in pieces:
        for s in range(sites):
            if c == 0:
                load_basis(t, s).start()
            load_fine(c, t, s).start()
        if c == 0 and t == 0:
            load_diag.start()
    load_hops.start()

    def remote(source, target, send, recv, device):
        return pltpu.make_async_remote_copy(
            src_ref=source, dst_ref=target, send_sem=send, recv_sem=recv,
            device_id=device, device_id_type=pl.DeviceIdType.MESH)

    def to_partner(x, c, t):
        return remote(cells.at[x, c, t], from_partner.at[x, c, t],
                      partner_send.at[x, c, t], partner_recv.at[x, c, t], (lat, partner))

    def to_far(x, c, t):
        return remote(from_partner.at[x, c, t], from_far.at[x, c, t],
                      far_send.at[x, c, t], far_recv.at[x, c, t], (lat, far_target))

    def to_later(x, c):
        return remote(cells.at[x, c, times - 1], below.at[x, c],
                      below_send.at[x, c], below_recv.at[x, c], (later, src))

    def to_earlier(x, c):
        return remote(cells.at[x, c, 0], above.at[x, c],
                      above_send.at[x, c], above_recv.at[x, c], (earlier, src))

    def send(x, c, t):
        to_partner(x, c, t).start()
        if t == times - 1:
            to_later(x, c).start()
        if t == 0:
            to_earlier(x, c).start()

    for c, t in pieces:
        coarse = []
        for s in range(sites):
            if c == 0:
                load_basis(t, s).wait()
            load_fine(c, t, s).wait()
            coarse.append(dot(fine_v[t, s, span(c)], basis_v[t, s]))
        if c == 0 and t == 0:
            load_diag.wait()
        swap = lax.rem(agg[t, 0], sites) == 1
        for s in range(sites):
            here = jnp.where(swap, coarse[1 - s], coarse[s]).astype(BF16)
            rhs[c, t, s] = here
            cells[0, c, t, s] = (DAMPING * dot(here, diag_v[t, s])).astype(BF16)
        if c == 0 and t == 0:
            pl.semaphore_wait(barrier, 4)
        send(0, c, t)
    load_hops.wait()

    def local_terms(x, c, t):
        for s in range(sites):
            own, other = cells[x, c, t, s], cells[x, c, t, 1 - s]
            total = dot(jnp.concatenate([own, own], axis=1), hops_v[t, s, 2:4].reshape(-1, own.shape[1]))
            total += dot(jnp.concatenate([other, other], axis=1), hops_v[t, s, 4:6].reshape(-1, own.shape[1]))
            if t + 1 < times:
                total += dot(cells[x, c, t + 1, s], hops_v[t, s, 6])
            if t > 0:
                total += dot(cells[x, c, t - 1, s], hops_v[t, s, 7])
            acc[c, t, s] = rhs[c, t, s].astype(F32) - total

    def forward(x, c, t):
        to_partner(x, c, t).wait_recv()
        to_far(x, c, t).start()

    def finish(x, c, t):
        if t == times - 1:
            to_earlier(x, c).wait_recv()
        if t == 0:
            to_later(x, c).wait_recv()
        to_far(x, c, t).wait_recv()
        for s in range(sites):
            site = src * sites + s
            near = partner * sites + s
            column = jnp.where(table[0, site] == near, 0, 1)
            total = dot(from_partner[x, c, t, s], hops_v[t, s, column])
            total += dot(from_far[x, c, t, s], hops_v[t, s, 1 - column])
            if t == times - 1:
                total += dot(above[x, c, s], hops_v[t, s, 6])
            if t == 0:
                total += dot(below[x, c, s], hops_v[t, s, 7])
            difference = (acc[c, t, s] - total).astype(BF16)
            applied = dot(difference, diag_v[t, s])
            new = ((1.0 - DAMPING) * cells[x, c, t, s].astype(F32) + DAMPING * applied).astype(BF16)
            if x + 1 < SWEEPS - 1:
                cells[x + 1, c, t, s] = new
            else:
                last[c, t, s] = new
        if x + 1 < SWEEPS - 1:
            send(x + 1, c, t)
            if t == times - 1:
                for each in range(times):
                    local_terms(x + 1, c, each)
        else:
            store(c, t).start()

    def store(c, t):
        return pltpu.make_async_copy(last.at[c, t], out.at[t, :, span(c)], out_sem.at[c, t])

    exchanges = SWEEPS - 1
    count = len(pieces)
    for step in range(count + LAG * (2 * exchanges - 1)):
        for x in range(exchanges):
            at = step - 2 * LAG * x
            if 0 <= at < count:
                forward(x, *pieces[at])
                if x == 0:
                    local_terms(0, *pieces[at])
            at -= LAG
            if 0 <= at < count:
                finish(x, *pieces[at])

    for c, t in pieces:
        for x in range(exchanges):
            to_partner(x, c, t).wait_send()
            to_far(x, c, t).wait_send()
            if t == times - 1:
                to_later(x, c).wait_send()
            if t == 0:
                to_earlier(x, c).wait_send()
        store(c, t).wait()


def prolong_kernel(agg, cells, basis, out, cells_v, basis_v, out_v, cells_sem, basis_sem, out_sem):
    times, sites, sources, _ = cells.shape
    blocks = [(t, s) for t in range(times) for s in range(sites)]
    parts = 2
    rows = sources // parts

    def load_basis(t, s):
        return pltpu.make_async_copy(basis.at[t, s], basis_v.at[t, s], basis_sem.at[t, s])

    def store(t, s, p):
        span = pl.ds(p * rows, rows)
        return pltpu.make_async_copy(out_v.at[t, s, span], out.at[t, s, span], out_sem.at[t, s, p])

    load_cells = pltpu.make_async_copy(cells, cells_v, cells_sem)
    load_cells.start()
    for t, s in blocks:
        load_basis(t, s).start()
    load_cells.wait()
    for t, s in blocks:
        load_basis(t, s).wait()
        coarse = lax.rem(agg[t, s], sites)
        for p in range(parts):
            span = pl.ds(p * rows, rows)
            out_v[t, s, span] = lax.dot_general(
                cells_v[t, coarse, span], basis_v[t, s], (((1,), (1,)), ((), ())),
                preferred_element_type=F32).astype(BF16)
            store(t, s, p).start()
    for t, s in blocks:
        for p in range(parts):
            store(t, s, p).wait()


def body(lats, srcs, fine, basis, diag, hops, table, agg):
    times, sites, sources, depth = fine.shape
    width = basis.shape[3]
    chunks, exchanges = CHUNKS, SWEEPS - 1
    rows = sources // chunks
    any_spec = pl.BlockSpec(memory_space=pl.ANY)
    smem_spec = pl.BlockSpec(memory_space=pltpu.SMEM)
    dma = pltpu.SemaphoreType.DMA
    piece = (sites, rows, width)
    per_piece, per_chunk = dma((exchanges, chunks, times)), dma((exchanges, chunks))
    cells = pl.pallas_call(
        functools.partial(sweep_kernel, chunks, lats, srcs),
        out_shape=jax.ShapeDtypeStruct((times, sites, sources, width), BF16),
        in_specs=[any_spec] * 4 + [smem_spec] * 2,
        out_specs=any_spec,
        scratch_shapes=[
            pltpu.VMEM(fine.shape, BF16),
            pltpu.VMEM(basis.shape, BF16),
            pltpu.VMEM(diag.shape, BF16),
            pltpu.VMEM(hops.shape, BF16),
            pltpu.VMEM((chunks, times) + piece, BF16),
            pltpu.VMEM((chunks, times) + piece, F32),
            pltpu.VMEM((exchanges, chunks, times) + piece, BF16),
            pltpu.VMEM((exchanges, chunks, times) + piece, BF16),
            pltpu.VMEM((exchanges, chunks, times) + piece, BF16),
            pltpu.VMEM((exchanges, chunks) + piece, BF16),
            pltpu.VMEM((exchanges, chunks) + piece, BF16),
            pltpu.VMEM((chunks, times) + piece, BF16),
            dma((chunks, times, sites)),
            dma((times, sites)),
            dma(()),
            dma(()),
            dma((chunks, times)),
            per_piece, per_piece, per_piece, per_piece,
            per_chunk, per_chunk, per_chunk, per_chunk,
        ],
        compiler_params=pltpu.CompilerParams(collective_id=0, has_side_effects=True),
        name="sweeps",
    )(fine, basis, diag, hops, table.T, agg)
    return pl.pallas_call(
        prolong_kernel,
        out_shape=jax.ShapeDtypeStruct(fine.shape, BF16),
        in_specs=[smem_spec, any_spec, any_spec],
        out_specs=any_spec,
        scratch_shapes=[
            pltpu.VMEM(cells.shape, BF16),
            pltpu.VMEM(basis.shape, BF16),
            pltpu.VMEM(fine.shape, BF16),
            dma(()),
            dma((times, sites)),
            dma((times, sites, 2)),
        ],
        name="prolong",
    )(agg, cells, basis)


def solution(mesh):
    return jax.shard_map(
        functools.partial(body, mesh.shape["lat"], mesh.shape["src"]),
        mesh=mesh,
        in_specs=(
            P("lat", "src", None, None),
            P("lat", "src", None, None),
            P("lat", "src", None, None),
            P("lat", "src", None, None, None),
            P(),
            P("lat", "src"),
        ),
        out_specs=P("lat", "src", None, None),
        check_vma=False,
    )
```

```python
import functools

import jax
import jax.numpy as jnp
from jax import lax
from jax.experimental import pallas as pl
from jax.experimental.pallas import tpu as pltpu
from jax.sharding import PartitionSpec as P

SWEEPS = 3
DAMPING = 0.8
CHUNKS = 4
LAG = 4
STORES = 2
F32 = jnp.float32
BF16 = jnp.bfloat16


def dot(a, b):
    return jnp.dot(a, b, preferred_element_type=F32)


def sweep_kernel(
    chunks, lats, srcs, fine, basis, diag, hops, table, agg, last, basis_v,
    fine_v, diag_v, hops_v, rhs, acc, cells, from_partner, from_far, above, below,
    fine_sem, basis_sem, diag_sem, hops_sem,
    partner_send, partner_recv, far_send, far_recv, above_send, above_recv, below_send, below_recv,
):
    times, sites, sources, _ = fine.shape
    rows = sources // chunks
    lat, src = lax.axis_index("lat"), lax.axis_index("src")
    later, earlier = lax.rem(lat + 1, lats), lax.rem(lat + lats - 1, lats)
    odd = lax.rem(src, 2)
    partner = src + 1 - 2 * odd
    far_target = lax.rem(src + 2 - 4 * odd + srcs, srcs)
    far_source = lax.rem(src - 2 + 4 * odd + srcs, srcs)

    barrier = pltpu.get_barrier_semaphore()
    for device in ((later, src), (earlier, src), (lat, partner), (lat, far_source)):
        pl.semaphore_signal(barrier, inc=1, device_id=device, device_id_type=pl.DeviceIdType.MESH)

    def span(c):
        return pl.ds(c * rows, rows)

    def load_fine(c, t, s):
        return pltpu.make_async_copy(
            fine.at[t, s, span(c)], fine_v.at[t, s, span(c)], fine_sem.at[c, t, s])

    def load_basis(t, s):
        return pltpu.make_async_copy(basis.at[t, s], basis_v.at[t, s], basis_sem.at[t, s])

    load_diag = pltpu.make_async_copy(diag, diag_v, diag_sem)
    load_hops = pltpu.make_async_copy(hops, hops_v, hops_sem)

    pieces = [(c, t) for t in range(times) for c in range(chunks)]
    for c, t in pieces:
        for s in range(sites):
            if c == 0:
                load_basis(t, s).start()
            load_fine(c, t, s).start()
        if c == 0 and t == 0:
            load_diag.start()
    load_hops.start()

    def remote(source, target, send, recv, device):
        return pltpu.make_async_remote_copy(
            src_ref=source, dst_ref=target, send_sem=send, recv_sem=recv,
            device_id=device, device_id_type=pl.DeviceIdType.MESH)

    def to_partner(x, c, t):
        return remote(cells.at[x, c, t], from_partner.at[x, c, t],
                      partner_send.at[x, c, t], partner_recv.at[x, c, t], (lat, partner))

    def to_far(x, c, t):
        return remote(from_partner.at[x, c, t], from_far.at[x, c, t],
                      far_send.at[x, c, t], far_recv.at[x, c, t], (lat, far_target))

    def to_later(x, c):
        return remote(cells.at[x, c, times - 1], below.at[x, c],
                      below_send.at[x, c], below_recv.at[x, c], (later, src))

    def to_earlier(x, c):
        return remote(cells.at[x, c, 0], above.at[x, c],
                      above_send.at[x, c], above_recv.at[x, c], (earlier, src))

    def send(x, c, t):
        to_partner(x, c, t).start()
        if t == times - 1:
            to_later(x, c).start()
        if t == 0:
            to_earlier(x, c).start()

    for c, t in pieces:
        for s in range(sites):
            if c == 0:
                load_basis(t, s).wait()
            load_fine(c, t, s).wait()
        if c == 0 and t == 0:
            load_diag.wait()
        coarse = [dot(fine_v[t, s, span(c)], basis_v[t, s]) for s in range(sites)]
        swap = lax.rem(agg[t, 0], sites) == 1
        here = [jnp.where(swap, coarse[1 - s], coarse[s]).astype(BF16) for s in range(sites)]
        applied = [dot(here[s], diag_v[t, s]) for s in range(sites)]
        for s in range(sites):
            cells[0, c, t, s] = (DAMPING * applied[s]).astype(BF16)
            rhs[c, t, s] = here[s]
        if c == 0 and t == 0:
            pl.semaphore_wait(barrier, 4)
        send(0, c, t)
    load_hops.wait()

    def local_terms(x, c, t):
        for s in range(sites):
            own, other = cells[x, c, t, s], cells[x, c, t, 1 - s]
            total = dot(jnp.concatenate([own, own], axis=1), hops_v[t, s, 2:4].reshape(-1, own.shape[1]))
            total += dot(jnp.concatenate([other, other], axis=1), hops_v[t, s, 4:6].reshape(-1, own.shape[1]))
            if t + 1 < times:
                total += dot(cells[x, c, t + 1, s], hops_v[t, s, 6])
            if t > 0:
                total += dot(cells[x, c, t - 1, s], hops_v[t, s, 7])
            acc[c, t, s] = rhs[c, t, s].astype(F32) - total

    def forward(x, c, t):
        to_partner(x, c, t).wait_recv()
        to_far(x, c, t).start()

    def finish(x, c, t):
        if t == times - 1:
            to_earlier(x, c).wait_recv()
        if t == 0:
            to_later(x, c).wait_recv()
        to_far(x, c, t).wait_recv()
        totals = []
        for s in range(sites):
            column = jnp.where(table[0, src * sites + s] == partner * sites + s, 0, 1)
            total = dot(from_partner[x, c, t, s], hops_v[t, s, column])
            total += dot(from_far[x, c, t, s], hops_v[t, s, 1 - column])
            if t == times - 1:
                total += dot(above[x, c, s], hops_v[t, s, 6])
            if t == 0:
                total += dot(below[x, c, s], hops_v[t, s, 7])
            totals.append(total)
        differences = [(acc[c, t, s] - totals[s]).astype(BF16) for s in range(sites)]
        applied = [dot(differences[s], diag_v[t, s]) for s in range(sites)]
        for s in range(sites):
            new = ((1.0 - DAMPING) * cells[x, c, t, s].astype(F32) + DAMPING * applied[s]).astype(BF16)
            if x + 1 < SWEEPS - 1:
                cells[x + 1, c, t, s] = new
            else:
                last[t, s, span(c)] = new
        if x + 1 < SWEEPS - 1:
            send(x + 1, c, t)
            if t == times - 1:
                for each in range(times):
                    local_terms(x + 1, c, each)

    exchanges = SWEEPS - 1
    count = len(pieces)
    for step in range(count + LAG * (2 * exchanges - 1)):
        for x in range(exchanges):
            at = step - 2 * LAG * x
            if 0 <= at < count:
                forward(x, *pieces[at])
                if x == 0:
                    local_terms(0, *pieces[at])
            at -= LAG
            if 0 <= at < count:
                finish(x, *pieces[at])

    for c, t in pieces:
        for x in range(exchanges):
            to_partner(x, c, t).wait_send()
            to_far(x, c, t).wait_send()
            if t == times - 1:
                to_later(x, c).wait_send()
            if t == 0:
                to_earlier(x, c).wait_send()


def prolong_kernel(agg, cells, basis, out, out_v, out_sem):
    times, sites, sources, _ = cells.shape
    blocks = [(t, s, p) for t in range(times) for s in range(sites) for p in range(STORES)]
    rows = sources // STORES

    def store(t, s, p):
        span = pl.ds(p * rows, rows)
        return pltpu.make_async_copy(out_v.at[t, s, span], out.at[t, s, span], out_sem.at[t, s, p])

    for t, s, p in blocks:
        span = pl.ds(p * rows, rows)
        out_v[t, s, span] = lax.dot_general(
            cells[t, lax.rem(agg[t, s], sites), span], basis[t, s], (((1,), (1,)), ((), ())),
            preferred_element_type=F32).astype(BF16)
        store(t, s, p).start()
    for t, s, p in blocks:
        store(t, s, p).wait()


def body(lats, srcs, fine, basis, diag, hops, table, agg):
    times, sites, sources, depth = fine.shape
    width = basis.shape[3]
    chunks, exchanges = CHUNKS, SWEEPS - 1
    rows = sources // chunks
    any_spec = pl.BlockSpec(memory_space=pl.ANY)
    vmem_spec = pl.BlockSpec(memory_space=pltpu.VMEM)
    smem_spec = pl.BlockSpec(memory_space=pltpu.SMEM)
    dma = pltpu.SemaphoreType.DMA
    piece = (sites, rows, width)
    per_piece, per_chunk = dma((exchanges, chunks, times)), dma((exchanges, chunks))
    cells, basis = pl.pallas_call(
        functools.partial(sweep_kernel, chunks, lats, srcs),
        out_shape=[pltpu.VMEM((times, sites, sources, width), BF16), pltpu.VMEM(basis.shape, BF16)],
        in_specs=[any_spec] * 4 + [smem_spec] * 2,
        out_specs=[vmem_spec] * 2,
        scratch_shapes=[
            pltpu.VMEM(fine.shape, BF16),
            pltpu.VMEM(diag.shape, BF16),
            pltpu.VMEM(hops.shape, BF16),
            pltpu.VMEM((chunks, times) + piece, BF16),
            pltpu.VMEM((chunks, times) + piece, F32),
            pltpu.VMEM((exchanges, chunks, times) + piece, BF16),
            pltpu.VMEM((exchanges, chunks, times) + piece, BF16),
            pltpu.VMEM((exchanges, chunks, times) + piece, BF16),
            pltpu.VMEM((exchanges, chunks) + piece, BF16),
            pltpu.VMEM((exchanges, chunks) + piece, BF16),
            dma((chunks, times, sites)),
            dma((times, sites)),
            dma(()),
            dma(()),
            per_piece, per_piece, per_piece, per_piece,
            per_chunk, per_chunk, per_chunk, per_chunk,
        ],
        compiler_params=pltpu.CompilerParams(collective_id=0, has_side_effects=True),
        name="sweeps",
    )(fine, basis, diag, hops, table.T, agg)
    cells = pltpu.with_memory_space_constraint(cells, pltpu.VMEM)
    basis = pltpu.with_memory_space_constraint(basis, pltpu.VMEM)
    return pl.pallas_call(
        prolong_kernel,
        out_shape=jax.ShapeDtypeStruct(fine.shape, BF16),
        in_specs=[smem_spec, vmem_spec, vmem_spec],
        out_specs=any_spec,
        scratch_shapes=[pltpu.VMEM(fine.shape, BF16), dma((times, sites, STORES))],
        name="prolong",
    )(agg, cells, basis)


def solution(mesh):
    return jax.shard_map(
        functools.partial(body, mesh.shape["lat"], mesh.shape["src"]),
        mesh=mesh,
        in_specs=(
            P("lat", "src", None, None),
            P("lat", "src", None, None),
            P("lat", "src", None, None),
            P("lat", "src", None, None, None),
            P(),
            P("lat", "src"),
        ),
        out_specs=P("lat", "src", None, None),
        check_vma=False,
    )
```

```python
import functools

import jax
import jax.numpy as jnp
from jax import lax
from jax.experimental import pallas as pl
from jax.experimental.pallas import tpu as pltpu
from jax.sharding import PartitionSpec as P

SWEEPS = 3
DAMPING = 0.8
CHUNKS = 2
LAG = 4
STORES = 2
F32 = jnp.float32
BF16 = jnp.bfloat16


def dot(a, b):
    return jnp.dot(a, b, preferred_element_type=F32)


def sweep_kernel(
    chunks, lats, srcs, fine, basis, diag, hops, table, agg, last, basis_v,
    fine_v, diag_v, hops_v, rhs, acc, cells, from_partner, from_far, above, below,
    fine_sem, basis_sem, diag_sem, hops_sem,
    partner_send, partner_recv, far_send, far_recv, above_send, above_recv, below_send, below_recv,
):
    times, sites, sources, _ = fine.shape
    rows = sources // chunks
    lat, src = lax.axis_index("lat"), lax.axis_index("src")
    later, earlier = lax.rem(lat + 1, lats), lax.rem(lat + lats - 1, lats)
    odd = lax.rem(src, 2)
    partner = src + 1 - 2 * odd
    far_target = lax.rem(src + 2 - 4 * odd + srcs, srcs)
    far_source = lax.rem(src - 2 + 4 * odd + srcs, srcs)

    barrier = pltpu.get_barrier_semaphore()
    for device in ((later, src), (earlier, src), (lat, partner), (lat, far_source)):
        pl.semaphore_signal(barrier, inc=1, device_id=device, device_id_type=pl.DeviceIdType.MESH)

    def span(c):
        return pl.ds(c * rows, rows)

    def load_fine(c, t, s):
        return pltpu.make_async_copy(
            fine.at[t, s, span(c)], fine_v.at[t, s, span(c)], fine_sem.at[c, t, s])

    def load_basis(t, s):
        return pltpu.make_async_copy(basis.at[t, s], basis_v.at[t, s], basis_sem.at[t, s])

    load_diag = pltpu.make_async_copy(diag, diag_v, diag_sem)
    load_hops = pltpu.make_async_copy(hops, hops_v, hops_sem)

    pieces = [(c, t) for t in range(times) for c in range(chunks)]
    for c, t in pieces:
        for s in range(sites):
            if c == 0:
                load_basis(t, s).start()
            load_fine(c, t, s).start()
        if c == 0 and t == 0:
            load_diag.start()
    load_hops.start()

    def remote(source, target, send, recv, device):
        return pltpu.make_async_remote_copy(
            src_ref=source, dst_ref=target, send_sem=send, recv_sem=recv,
            device_id=device, device_id_type=pl.DeviceIdType.MESH)

    def to_partner(x, c, t):
        return remote(cells.at[x, c, t], from_partner.at[x, c, t],
                      partner_send.at[x, c, t], partner_recv.at[x, c, t], (lat, partner))

    def to_far(x, c, t):
        return remote(from_partner.at[x, c, t], from_far.at[x, c, t],
                      far_send.at[x, c, t], far_recv.at[x, c, t], (lat, far_target))

    def to_later(x, c):
        return remote(cells.at[x, c, times - 1], below.at[x, c],
                      below_send.at[x, c], below_recv.at[x, c], (later, src))

    def to_earlier(x, c):
        return remote(cells.at[x, c, 0], above.at[x, c],
                      above_send.at[x, c], above_recv.at[x, c], (earlier, src))

    def send(x, c, t):
        to_partner(x, c, t).start()
        if t == times - 1:
            to_later(x, c).start()
        if t == 0:
            to_earlier(x, c).start()

    for c, t in pieces:
        for s in range(sites):
            if c == 0:
                load_basis(t, s).wait()
            load_fine(c, t, s).wait()
        if c == 0 and t == 0:
            load_diag.wait()
        coarse = [dot(fine_v[t, s, span(c)], basis_v[t, s]) for s in range(sites)]
        swap = lax.rem(agg[t, 0], sites) == 1
        here = [jnp.where(swap, coarse[1 - s], coarse[s]).astype(BF16) for s in range(sites)]
        applied = [dot(here[s], diag_v[t, s]) for s in range(sites)]
        for s in range(sites):
            cells[0, c, t, s] = (DAMPING * applied[s]).astype(BF16)
            rhs[c, t, s] = here[s]
        if c == 0 and t == 0:
            pl.semaphore_wait(barrier, 4)
        send(0, c, t)
    load_hops.wait()

    def local_terms(x, c, t):
        for s in range(sites):
            own, other = cells[x, c, t, s], cells[x, c, t, 1 - s]
            total = dot(jnp.concatenate([own, own], axis=1), hops_v[t, s, 2:4].reshape(-1, own.shape[1]))
            total += dot(jnp.concatenate([other, other], axis=1), hops_v[t, s, 4:6].reshape(-1, own.shape[1]))
            if t + 1 < times:
                total += dot(cells[x, c, t + 1, s], hops_v[t, s, 6])
            if t > 0:
                total += dot(cells[x, c, t - 1, s], hops_v[t, s, 7])
            acc[c, t, s] = rhs[c, t, s].astype(F32) - total

    def forward(x, c, t):
        to_partner(x, c, t).wait_recv()
        to_far(x, c, t).start()

    def finish(x, c, t):
        if t == times - 1:
            to_earlier(x, c).wait_recv()
        if t == 0:
            to_later(x, c).wait_recv()
        to_far(x, c, t).wait_recv()
        totals = []
        for s in range(sites):
            column = jnp.where(table[0, src * sites + s] == partner * sites + s, 0, 1)
            total = dot(from_partner[x, c, t, s], hops_v[t, s, column])
            total += dot(from_far[x, c, t, s], hops_v[t, s, 1 - column])
            if t == times - 1:
                total += dot(above[x, c, s], hops_v[t, s, 6])
            if t == 0:
                total += dot(below[x, c, s], hops_v[t, s, 7])
            totals.append(total)
        differences = [(acc[c, t, s] - totals[s]).astype(BF16) for s in range(sites)]
        applied = [dot(differences[s], diag_v[t, s]) for s in range(sites)]
        for s in range(sites):
            new = ((1.0 - DAMPING) * cells[x, c, t, s].astype(F32) + DAMPING * applied[s]).astype(BF16)
            if x + 1 < SWEEPS - 1:
                cells[x + 1, c, t, s] = new
            else:
                last[t, s, span(c)] = new
        if x + 1 < SWEEPS - 1:
            send(x + 1, c, t)
            if t == times - 1:
                for each in range(times):
                    local_terms(x + 1, c, each)

    exchanges = SWEEPS - 1
    count = len(pieces)
    for step in range(count + LAG * (2 * exchanges - 1)):
        for x in range(exchanges):
            at = step - 2 * LAG * x
            if 0 <= at < count:
                forward(x, *pieces[at])
                if x == 0:
                    local_terms(0, *pieces[at])
            at -= LAG
            if 0 <= at < count:
                finish(x, *pieces[at])

    for c, t in pieces:
        for x in range(exchanges):
            to_partner(x, c, t).wait_send()
            to_far(x, c, t).wait_send()
            if t == times - 1:
                to_later(x, c).wait_send()
            if t == 0:
                to_earlier(x, c).wait_send()


def prolong_kernel(agg, cells, basis, out, out_v, out_sem):
    times, sites, sources, _ = cells.shape
    blocks = [(t, s, p) for t in range(times) for s in range(sites) for p in range(STORES)]
    rows = sources // STORES

    def store(t, s, p):
        span = pl.ds(p * rows, rows)
        return pltpu.make_async_copy(out_v.at[t, s, span], out.at[t, s, span], out_sem.at[t, s, p])

    for t, s, p in blocks:
        span = pl.ds(p * rows, rows)
        out_v[t, s, span] = lax.dot_general(
            cells[t, lax.rem(agg[t, s], sites), span], basis[t, s], (((1,), (1,)), ((), ())),
            preferred_element_type=F32).astype(BF16)
        store(t, s, p).start()
    for t, s, p in blocks:
        store(t, s, p).wait()


def body(lats, srcs, fine, basis, diag, hops, table, agg):
    times, sites, sources, depth = fine.shape
    width = basis.shape[3]
    chunks, exchanges = CHUNKS, SWEEPS - 1
    rows = sources // chunks
    any_spec = pl.BlockSpec(memory_space=pl.ANY)
    vmem_spec = pl.BlockSpec(memory_space=pltpu.VMEM)
    smem_spec = pl.BlockSpec(memory_space=pltpu.SMEM)
    dma = pltpu.SemaphoreType.DMA
    piece = (sites, rows, width)
    per_piece, per_chunk = dma((exchanges, chunks, times)), dma((exchanges, chunks))
    cells, basis = pl.pallas_call(
        functools.partial(sweep_kernel, chunks, lats, srcs),
        out_shape=[pltpu.VMEM((times, sites, sources, width), BF16), pltpu.VMEM(basis.shape, BF16)],
        in_specs=[any_spec] * 4 + [smem_spec] * 2,
        out_specs=[vmem_spec] * 2,
        scratch_shapes=[
            pltpu.VMEM(fine.shape, BF16),
            pltpu.VMEM(diag.shape, BF16),
            pltpu.VMEM(hops.shape, BF16),
            pltpu.VMEM((chunks, times) + piece, BF16),
            pltpu.VMEM((chunks, times) + piece, F32),
            pltpu.VMEM((exchanges, chunks, times) + piece, BF16),
            pltpu.VMEM((exchanges, chunks, times) + piece, BF16),
            pltpu.VMEM((exchanges, chunks, times) + piece, BF16),
            pltpu.VMEM((exchanges, chunks) + piece, BF16),
            pltpu.VMEM((exchanges, chunks) + piece, BF16),
            dma((chunks, times, sites)),
            dma((times, sites)),
            dma(()),
            dma(()),
            per_piece, per_piece, per_piece, per_piece,
            per_chunk, per_chunk, per_chunk, per_chunk,
        ],
        compiler_params=pltpu.CompilerParams(collective_id=0, has_side_effects=True),
        name="sweeps",
    )(fine, basis, diag, hops, table.T, agg)
    cells = pltpu.with_memory_space_constraint(cells, pltpu.VMEM)
    basis = pltpu.with_memory_space_constraint(basis, pltpu.VMEM)
    return pl.pallas_call(
        prolong_kernel,
        out_shape=jax.ShapeDtypeStruct(fine.shape, BF16),
        in_specs=[smem_spec, vmem_spec, vmem_spec],
        out_specs=any_spec,
        scratch_shapes=[pltpu.VMEM(fine.shape, BF16), dma((times, sites, STORES))],
        name="prolong",
    )(agg, cells, basis)


def solution(mesh):
    return jax.shard_map(
        functools.partial(body, mesh.shape["lat"], mesh.shape["src"]),
        mesh=mesh,
        in_specs=(
            P("lat", "src", None, None),
            P("lat", "src", None, None),
            P("lat", "src", None, None),
            P("lat", "src", None, None, None),
            P(),
            P("lat", "src"),
        ),
        out_specs=P("lat", "src", None, None),
        check_vma=False,
    )
```
